32 devices in a mesh: tm: 32 (over z, y, x, core), panel: 1.
Axes of the slice: x: 2, y: 2, z: 4, core: 2. Of those that a mesh axis runs over, the one named last changes fastest.
Arguments:
- observations: float32 [1024, 64], P('tm'), may hold values from -600 to 600
- obs_weights: float32 [1024, 64], P('tm'), may hold values from 0 to 1
- damping: float32 [1024, 256], P('tm'), may hold values from 0.1 to 1
- transition: float32 [256, 256], replicated, may hold values from -1 to 1
- obs_matrix: float32 [64, 256], replicated, may hold values from -0.25 to 0.25
- smoother_gain: float32 [256, 256], replicated, may hold values from -1 to 1
- prior_mean: float32 [256], replicated, may hold values from -6 to 6
Outputs:
- filtered: float32 [1024, 256], P('tm')
- smoothed: float32 [1024, 256], P('tm')
The draws below stay inside these ranges and needn't reach their ends.
All inputs are finite; a program needn't handle non-finite values.
Results may differ from the reference program's by a relative error of at most 0.0003.
Values sent between devices are 32-bit elements; how exact they have to be, the bound alone decides.
A program may use at most 64 MiB of HBM per device.

```python
import jax
import jax.numpy as jnp
from jax import lax

NS = 256
OBS = 64
STEPS_DEV = 32
STEPS = 1024


highest = lax.Precision.HIGHEST


def rotation_matrix(key, spread):
    raw = jax.random.normal(key, (NS, NS), jnp.float32) / jnp.sqrt(jnp.float32(NS))
    skewed = (raw - raw.T) * (0.5 * spread) / 256.0
    identity = jnp.eye(NS, dtype=jnp.float32)
    term_matrix = identity
    total_matrix = identity
    for order_index in range(1, 11):
        term_matrix = jnp.dot(term_matrix, skewed, precision=highest) / float(order_index)
        total_matrix = total_matrix + term_matrix
    for square_index in range(8):
        total_matrix = jnp.dot(total_matrix, total_matrix, precision=highest)
    return total_matrix


def draw_transition(key, part):
    spread = 0.4
    return rotation_matrix(jax.random.fold_in(key, 101), spread)


def draw_smoother_gain(key, part):
    spread = 0.4
    rate_low = 0.05
    rate_high = 2.0
    base_matrix = rotation_matrix(jax.random.fold_in(key, 101), spread)
    rates = jnp.exp(jax.random.uniform(jax.random.fold_in(key, 202), (NS,), jnp.float32, jnp.log(rate_low), jnp.log(rate_high)))
    keeps = jnp.exp(-rates / float(STEPS))
    return base_matrix.T * keeps[None, :]


def draw_damping(key, part):
    rate_low = 0.05
    rate_high = 2.0
    channel_rates = jnp.exp(jax.random.uniform(jax.random.fold_in(key, 301), (NS,), jnp.float32, jnp.log(rate_low), jnp.log(rate_high)))
    block_rates = jnp.exp(jax.random.uniform(jax.random.fold_in(key, 302), (STEPS // STEPS_DEV, 1), jnp.float32, jnp.log(0.5), jnp.log(2.0)))
    block_rates = jnp.repeat(block_rates, STEPS_DEV, axis=0)
    roughness = jnp.exp(jax.random.uniform(jax.random.fold_in(key, 303), (STEPS, NS), jnp.float32, jnp.log(0.5), jnp.log(2.0)))
    rates = channel_rates[None, :] * block_rates * roughness / float(STEPS)
    positions = jax.random.randint(jax.random.fold_in(key, 304), (3,), 0, STEPS)
    strengths = jax.random.uniform(jax.random.fold_in(key, 305), (3,), jnp.float32, 0.5, 0.8)
    step_ids = lax.broadcasted_iota(jnp.int32, (STEPS, 3), 0)
    factors = jnp.prod(jnp.where(step_ids == positions[None, :], strengths[None, :], 1.0), axis=1)
    return jnp.exp(-rates) * factors[:, None]


def draw_obs_weights(key, part):
    scale_value = float(NS) / float(OBS * STEPS)
    values = jnp.exp(jax.random.uniform(jax.random.fold_in(key, 401), (STEPS, OBS), jnp.float32, jnp.log(0.1), jnp.log(3.0)))
    return values * scale_value


def steps_of(own_key, dims, pieces, low, top_value):
    loudness, own = 1.0, jax.random.fold_in(own_key, 6)
    for axis_at, shards_of in pieces:
        draws = jnp.exp(jax.random.uniform(jax.random.fold_in(own, axis_at), (shards_of,), jnp.float32, low / len(pieces), top_value / len(pieces)))
        loudness = loudness * jnp.repeat(draws, dims[axis_at] // shards_of).reshape([-1 if axis == axis_at else 1 for axis in range(len(dims))])
    return loudness


def gaussian(rng, extent, scale, reach, pieces=(), kind=jnp.bfloat16):
    drawn = jax.random.normal(rng, extent, jnp.float32) * scale
    if len(pieces) > 0:
        drawn = steps_of(rng, extent, pieces, -0.22, 0.18) * drawn
    return jnp.clip(drawn, min=-reach, max=reach).astype(kind)


def setup_inputs(seed: int = 0) -> dict:
    key_list = jax.random.split(jax.random.key(seed), 8)
    return {
        "observations": gaussian(key_list[0], (STEPS, OBS), 100.0, 600.0, ((0, 32),), jnp.float32),
        "obs_weights": draw_obs_weights(jax.random.fold_in(key_list[7], 71), 0),
        "damping": draw_damping(jax.random.fold_in(key_list[7], 71), 0),
        "transition": draw_transition(jax.random.fold_in(key_list[7], 71), 0),
        "obs_matrix": gaussian(key_list[4], (OBS, NS), (2 * NS) ** -0.5, 0.25, (), jnp.float32),
        "smoother_gain": draw_smoother_gain(jax.random.fold_in(key_list[7], 71), 0),
        "prior_mean": gaussian(key_list[6], (NS,), 1.0, 6.0, (), jnp.float32),
    }


highest = lax.Precision.HIGHEST


def product(left, right):
    return jnp.dot(left, right, precision=highest, preferred_element_type=jnp.float32)


def reference(observations, obs_weights, damping, transition, obs_matrix, smoother_gain, prior_mean):
    def update(predicted, obs_row, weight_row):
        innovation = obs_row - product(obs_matrix, predicted)
        return predicted + product(weight_row * innovation, obs_matrix)

    first_mean = update(prior_mean, observations[0], obs_weights[0])

    def forward_step(estimate, inputs):
        obs_row, weight_row, damp_row = inputs
        predicted = product(transition, damp_row * estimate)
        estimate = update(predicted, obs_row, weight_row)
        return estimate, estimate

    _, later_means = lax.scan(forward_step, first_mean, (observations[1:], obs_weights[1:], damping[1:]))
    filtered = jnp.concatenate([first_mean[None, :], later_means], axis=0)

    def backward_step(estimate, mean_row):
        estimate = mean_row + product(smoother_gain, estimate - product(transition, mean_row))
        return estimate, estimate

    _, earlier_smooth = lax.scan(backward_step, filtered[-1], filtered[:-1], reverse=True)
    smoothed = jnp.concatenate([earlier_smooth, filtered[-1:]], axis=0)
    return filtered, smoothed
```

```python
import functools

import jax
import jax.numpy as jnp
from jax import lax
from jax.experimental import pallas as pl
from jax.experimental.pallas import tpu as pltpu
from jax.sharding import PartitionSpec as P

F32 = jnp.float32
BF16 = jnp.bfloat16
PAD = 8
PIECES = 4


def halves(value):
    high = value.astype(BF16)
    return high, (value - high.astype(F32)).astype(BF16)


def split_lhs(value):
    high, low = halves(value)
    return jnp.concatenate([high, low, high], axis=1)


def split_rhs(value):
    high, low = halves(value)
    return jnp.concatenate([high, high, low], axis=0)


def dot3(left, right_split):
    return jnp.dot(split_lhs(left), right_split, preferred_element_type=F32)


def exact(left, right):
    return jnp.dot(left, right, precision=lax.Precision.HIGHEST, preferred_element_type=F32)


def matvec(row, matrix):
    width = matrix.shape[1]
    column = jnp.transpose(jnp.broadcast_to(row, (128, row.shape[1])))
    parts = [
        jnp.sum(column * matrix[:, at : at + 128], axis=0, keepdims=True)
        for at in range(0, width, 128)
    ]
    return jnp.concatenate(parts, axis=1)


def kernel(
    count, y_ref, w_ref, d_ref, t_ref, h_ref, g_ref, p_ref, f_ref, s_ref,
    node, current, arrived, gpow, gsplit, tt, kt, hs, dnext, evec, uvec,
    xin, xend, chain, obuf, gath,
    mat_send, mat_recv, chain_send, chain_recv, shift_send, shift_recv, o_send, o_recv,
):
    steps, width = d_ref.shape
    depth = steps.bit_length() - 1
    span_bits = (count - 1).bit_length()
    levels = min(3, span_bits)
    window = 1 << levels
    powers = depth + span_bits
    me = lax.axis_index("tm")
    is_first = jnp.where(me == 0, 1.0, 0.0).astype(F32)
    is_final = jnp.where(me == count - 1, 1.0, 0.0).astype(F32)

    gath[...] = jnp.zeros_like(gath)
    xin[...] = jnp.zeros_like(xin)
    barrier = pltpu.get_barrier_semaphore()
    for ahead in range(1, count):
        pl.semaphore_signal(
            barrier, inc=1, device_id={"tm": lax.rem(me + ahead, count)},
            device_id_type=pl.DeviceIdType.MESH,
        )

    h = h_ref[...]
    ht = jnp.transpose(h)
    t_trans = jnp.transpose(t_ref[...])
    tt[...] = t_trans
    kt[...] = exact(t_trans, ht)
    hs[...] = split_rhs(h)
    damp = d_ref[...]
    dnext[...] = jnp.concatenate([damp[1:], jnp.ones((1, width), F32)], axis=0)
    row_ids = lax.broadcasted_iota(jnp.int32, (steps, 1), 0)
    first_row = jnp.where(row_ids == 0, 1.0, 0.0).astype(F32) * is_first
    prior = p_ref[...]
    weights = w_ref[...]
    shifted = y_ref[...] - first_row * exact(jnp.broadcast_to(prior, (8, width)), ht)[0:1]
    evec[...] = (exact(weights * shifted, h) + first_row * prior) * dnext[...]
    pad_first = lax.broadcasted_iota(jnp.int32, (PAD, width), 0) == 0

    def leaf(step, carry):
        row = pl.ds(step, 1)
        drop = dot3(kt[...] * w_ref[row, :], hs[...])
        node[step, 0:width, :] = (tt[...] - drop) * dnext[row, :]
        node[step, width:, :] = jnp.where(pad_first, evec[row, :], 0.0)
        return carry

    lax.fori_loop(0, steps, leaf, 0, unroll=2)

    def combine(left, right):
        joined = dot3(left, split_rhs(right[0:width]))
        tail = joined[width:] + right[width:]
        return joined[0:width], tail

    def join_group(first, size):
        results = [
            combine(node[2 * (first + k)], node[2 * (first + k) + 1]) for k in range(size)
        ]
        for k, (body, tail) in enumerate(results):
            node[steps + first + k, 0:width, :] = body
            node[steps + first + k, width:, :] = tail

    pairs = (steps - 2) // 2

    def join_pair(index, carry):
        join_group(2 * index, 2)
        return carry

    lax.fori_loop(0, pairs, join_pair, 0)
    join_group(steps - 2, 1)

    root = 2 * steps - 2
    damp_col = jnp.transpose(jnp.broadcast_to(damp[0:1] * (1.0 - is_first), (128, width)))
    for at in range(0, width, 128):
        current[0, 0:width, at : at + 128] = node[root, 0:width, at : at + 128] * damp_col
    current[0, width:, :] = node[root, width:, :]

    pl.semaphore_wait(barrier, count - 1)

    def square(index, carry):
        base = gpow[index]
        gpow[index + 1] = exact(base, base)
        return carry

    gpow[0] = jnp.transpose(g_ref[...])
    piece = width // PIECES
    spans = [(k * piece, piece + (PAD if k == PIECES - 1 else 0)) for k in range(PIECES)]

    def matrix_copy(level, part):
        rows = pl.ds(*spans[part])
        return pltpu.make_async_remote_copy(
            src_ref=current.at[level, rows], dst_ref=arrived.at[level, rows],
            send_sem=mat_send.at[level, part], recv_sem=mat_recv.at[level, part],
            device_id={"tm": lax.rem(me + (1 << level), count)},
            device_id_type=pl.DeviceIdType.MESH,
        )

    def send_part(level, part):
        @pl.when(me + (1 << level) < count)
        def _():
            matrix_copy(level, part).start()

    for part in range(PIECES):
        send_part(0, part)
    done = 0
    for level in range(levels):
        reach = 1 << level
        until = (powers - 1) * (level + 1) // levels
        lax.fori_loop(done, until, square, 0)
        done = until

        @pl.when(me < reach)
        def _(level=level):
            current[level + 1] = current[level]

        for part, (start, size) in enumerate(spans):

            @pl.when(me >= reach)
            def _(level=level, part=part, start=start, size=size):
                matrix_copy(level, part).wait_recv()
                joined = dot3(
                    arrived[level, start : start + size, :],
                    split_rhs(current[level, 0:width, :]),
                )
                if part < PIECES - 1:
                    current[level + 1, start : start + size, :] = joined
                else:
                    current[level + 1, start:width, :] = joined[0:piece]
                    current[level + 1, width:, :] = joined[piece:] + current[level, width:, :]

            if level + 1 < levels:
                send_part(level + 1, part)

    chain_copy = pltpu.make_async_remote_copy(
        src_ref=xend, dst_ref=chain, send_sem=chain_send, recv_sem=chain_recv,
        device_id={"tm": lax.rem(me + window, count)}, device_id_type=pl.DeviceIdType.MESH,
    )
    shift_copy = pltpu.make_async_remote_copy(
        src_ref=xend, dst_ref=xin, send_sem=shift_send, recv_sem=shift_recv,
        device_id={"tm": lax.rem(me + 1, count)}, device_id_type=pl.DeviceIdType.MESH,
    )

    def pass_on():
        @pl.when(me + window < count)
        def _():
            chain_copy.start()

        @pl.when(me + 1 < count)
        def _():
            shift_copy.start()

    @pl.when(me < window)
    def _():
        xend[...] = current[levels, width : width + 1, :]
        pass_on()

    def keep(index, carry):
        gsplit[index] = split_rhs(gpow[index])
        return carry

    lax.fori_loop(0, powers, keep, 0)

    @pl.when(me >= window)
    def _():
        chain_copy.wait_recv()
        xend[...] = (
            matvec(chain[...], current[levels, 0:width, :])
            + current[levels, width : width + 1, :]
        )
        pass_on()

    for level in range(levels):
        for part in range(PIECES):

            @pl.when(me + (1 << level) < count)
            def _(level=level, part=part):
                matrix_copy(level, part).wait_send()

    @pl.when(me + window < count)
    def _():
        chain_copy.wait_send()

    @pl.when(me >= 1)
    def _():
        shift_copy.wait_recv()

    @pl.when(me + 1 < count)
    def _():
        shift_copy.wait_send()

    uvec[0] = xin[...] * damp[0:1]
    for level in range(depth - 1, -1, -1):
        size = 1 << level
        offset = 2 * steps - (2 * steps >> level)

        def descend(index, carry, size=size, offset=offset):
            enter = uvec[2 * size * index]
            left = offset + 2 * index
            uvec[2 * size * index + size] = (
                matvec(enter, node[left, 0:width, :]) + node[left, width : width + 1, :]
            )
            return carry

        trips = steps // (2 * size)
        lax.fori_loop(0, trips, descend, 0, unroll=min(4, trips))

    before = jnp.concatenate([uvec[step] for step in range(steps)], axis=0)
    predicted = exact(before, tt[...]) + first_row * prior
    innovation = y_ref[...] - exact(predicted, ht)
    filtered = predicted + exact(weights * innovation, h)
    f_ref[...] = filtered

    last_row = jnp.where(row_ids == steps - 1, 1.0, 0.0).astype(F32) * is_final
    base = filtered - (1.0 - last_row) * exact(exact(filtered, tt[...]), gpow[0])
    for level in range(depth):
        distance = 1 << level
        later = jnp.concatenate(
            [base[distance:], jnp.zeros((distance, width), F32)], axis=0
        )
        base = base + dot3(later, gsplit[level])
    obuf[...] = base[0:1]
    copies = []
    for rank in range(count - 1):
        copy = pltpu.make_async_remote_copy(
            src_ref=obuf, dst_ref=gath.at[rank], send_sem=o_send.at[rank],
            recv_sem=o_recv.at[rank],
            device_id={"tm": lax.rem(me + 2 * count - 1 - rank, count)},
            device_id_type=pl.DeviceIdType.MESH,
        )
        copies.append(copy)

        @pl.when(me > rank)
        def _(copy=copy):
            copy.start()

    for rank, copy in enumerate(copies):

        @pl.when(me + rank + 1 < count)
        def _(copy=copy):
            copy.wait_recv()

    gathered = jnp.concatenate([gath[rank] for rank in range(gath.shape[0])], axis=0)
    for level in range(span_bits - 1, -1, -1):
        half = 1 << level
        gathered = gathered[0:half] + dot3(gathered[half:], gsplit[depth + level])
    lifted = dot3(gathered, gsplit[0])
    for level in range(depth):
        lifted = jnp.concatenate([dot3(lifted, gsplit[level]), lifted], axis=0)
    s_ref[...] = base + lifted

    for rank, copy in enumerate(copies):

        @pl.when(me > rank)
        def _(copy=copy):
            copy.wait_send()


def per_device(
    observations, obs_weights, damping, transition, obs_matrix, smoother_gain, prior_mean
):
    count = lax.axis_size("tm")
    steps, width = damping.shape
    obs = observations.shape[1]
    span_bits = (count - 1).bit_length()
    levels = min(3, span_bits)
    powers = steps.bit_length() - 1 + span_bits
    vmem = pl.BlockSpec(memory_space=pltpu.VMEM)
    out = jax.ShapeDtypeStruct((steps, width), F32)
    dma = pltpu.SemaphoreType.DMA
    return pl.pallas_call(
        functools.partial(kernel, count),
        out_shape=(out, out),
        in_specs=[vmem] * 7,
        out_specs=(vmem, vmem),
        scratch_shapes=[
            pltpu.VMEM((2 * steps - 1, width + PAD, width), F32),
            pltpu.VMEM((levels + 1, width + PAD, width), F32),
            pltpu.VMEM((levels, width + PAD, width), F32),
            pltpu.VMEM((powers, width, width), F32),
            pltpu.VMEM((powers, 3 * width, width), BF16),
            pltpu.VMEM((width, width), F32),
            pltpu.VMEM((width, obs), F32),
            pltpu.VMEM((3 * obs, width), BF16),
            pltpu.VMEM((steps, width), F32),
            pltpu.VMEM((steps, width), F32),
            pltpu.VMEM((steps, 1, width), F32),
            pltpu.VMEM((1, width), F32),
            pltpu.VMEM((1, width), F32),
            pltpu.VMEM((1, width), F32),
            pltpu.VMEM((1, width), F32),
            pltpu.VMEM((1 << span_bits, 1, width), F32),
            dma((levels, PIECES)), dma((levels, PIECES)),
            dma, dma, dma, dma,
            dma((count - 1,)), dma((count - 1,)),
        ],
        compiler_params=pltpu.CompilerParams(
            collective_id=0, has_side_effects=True, vmem_limit_bytes=56 * 1024 * 1024
        ),
    )(
        observations, obs_weights, damping, transition, obs_matrix, smoother_gain,
        prior_mean[None, :],
    )


def solution(mesh):
    return jax.shard_map(
        per_device,
        mesh=mesh,
        in_specs=(P("tm", None), P("tm", None), P("tm", None), P(), P(), P(), P()),
        out_specs=(P("tm", None), P("tm", None)),
        check_vma=False,
    )
```

```python
import functools

import jax
import jax.numpy as jnp
from jax import lax
from jax.experimental import pallas as pl
from jax.experimental.pallas import tpu as pltpu
from jax.sharding import PartitionSpec as P

F32 = jnp.float32
BF16 = jnp.bfloat16
PAD = 8
PIECES = 4


def halves(value):
    high = value.astype(BF16)
    return high, (value - high.astype(F32)).astype(BF16)


def split_lhs(value):
    high, low = halves(value)
    return jnp.concatenate([high, low, high], axis=1)


def split_rhs(value):
    high, low = halves(value)
    return jnp.concatenate([high, high, low], axis=0)


def dot3(left, right_split):
    return jnp.dot(split_lhs(left), right_split, preferred_element_type=F32)


def exact(left, right):
    return jnp.dot(left, right, precision=lax.Precision.HIGHEST, preferred_element_type=F32)


def matvec(row, matrix):
    width = matrix.shape[1]
    column = jnp.transpose(jnp.broadcast_to(row, (128, row.shape[1])))
    parts = [
        jnp.sum(column * matrix[:, at : at + 128], axis=0, keepdims=True)
        for at in range(0, width, 128)
    ]
    return jnp.concatenate(parts, axis=1)


def kernel(
    count, y_ref, w_ref, d_ref, t_ref, h_ref, g_ref, p_ref, f_ref, s_ref,
    node, current, arrived, gpow, gsplit, tt, kt, hs, dnext, evec, uvec,
    xin, xend, chain, obuf, gath,
    mat_send, mat_recv, chain_send, chain_recv, shift_send, shift_recv, o_send, o_recv,
):
    steps, width = d_ref.shape
    depth = steps.bit_length() - 1
    span_bits = (count - 1).bit_length()
    levels = min(3, span_bits)
    window = 1 << levels
    powers = depth + span_bits
    me = lax.axis_index("tm")
    is_first = jnp.where(me == 0, 1.0, 0.0).astype(F32)
    is_final = jnp.where(me == count - 1, 1.0, 0.0).astype(F32)

    gath[...] = jnp.zeros_like(gath)
    xin[...] = jnp.zeros_like(xin)
    barrier = pltpu.get_barrier_semaphore()
    for ahead in range(1, count):
        pl.semaphore_signal(
            barrier, inc=1, device_id={"tm": lax.rem(me + ahead, count)},
            device_id_type=pl.DeviceIdType.MESH,
        )

    h = h_ref[...]
    ht = jnp.transpose(h)
    t_trans = jnp.transpose(t_ref[...])
    tt[...] = t_trans
    kt[...] = exact(t_trans, ht)
    hs[...] = split_rhs(h)
    damp = d_ref[...]
    dnext[...] = jnp.concatenate([damp[1:], jnp.ones((1, width), F32)], axis=0)
    row_ids = lax.broadcasted_iota(jnp.int32, (steps, 1), 0)
    first_row = jnp.where(row_ids == 0, 1.0, 0.0).astype(F32) * is_first
    prior = p_ref[...]
    weights = w_ref[...]
    shifted = y_ref[...] - first_row * exact(jnp.broadcast_to(prior, (8, width)), ht)[0:1]
    evec[...] = (exact(weights * shifted, h) + first_row * prior) * dnext[...]
    pad_first = lax.broadcasted_iota(jnp.int32, (PAD, width), 0) == 0

    def leaf(step, carry):
        row = pl.ds(step, 1)
        drop = dot3(kt[...] * w_ref[row, :], hs[...])
        node[step, 0:width, :] = (tt[...] - drop) * dnext[row, :]
        node[step, width:, :] = jnp.where(pad_first, evec[row, :], 0.0)
        return carry

    lax.fori_loop(0, steps, leaf, 0, unroll=2)

    def combine(left, right):
        joined = dot3(left, split_rhs(right[0:width]))
        tail = joined[width:] + right[width:]
        return joined[0:width], tail

    def join_group(first, size):
        results = [
            combine(node[2 * (first + k)], node[2 * (first + k) + 1]) for k in range(size)
        ]
        for k, (body, tail) in enumerate(results):
            node[steps + first + k, 0:width, :] = body
            node[steps + first + k, width:, :] = tail

    pairs = (steps - 2) // 2

    def join_pair(index, carry):
        join_group(2 * index, 2)
        return carry

    lax.fori_loop(0, pairs, join_pair, 0)
    join_group(steps - 2, 1)

    root = 2 * steps - 2
    damp_col = jnp.transpose(jnp.broadcast_to(damp[0:1] * (1.0 - is_first), (128, width)))
    for at in range(0, width, 128):
        current[0, 0:width, at : at + 128] = node[root, 0:width, at : at + 128] * damp_col
    current[0, width:, :] = node[root, width:, :]

    pl.semaphore_wait(barrier, count - 1)

    def square(index, carry):
        base = gpow[index]
        gpow[index + 1] = exact(base, base)
        return carry

    gpow[0] = jnp.transpose(g_ref[...])
    piece = width // PIECES
    spans = [(k * piece, piece + (PAD if k == PIECES - 1 else 0)) for k in range(PIECES)]

    def matrix_copy(level, part):
        rows = pl.ds(*spans[part])
        return pltpu.make_async_remote_copy(
            src_ref=current.at[level, rows], dst_ref=arrived.at[level, rows],
            send_sem=mat_send.at[level, part], recv_sem=mat_recv.at[level, part],
            device_id={"tm": lax.rem(me + (1 << level), count)},
            device_id_type=pl.DeviceIdType.MESH,
        )

    def send_part(level, part):
        @pl.when(me + (1 << level) < count)
        def _():
            matrix_copy(level, part).start()

    for part in range(PIECES):
        send_part(0, part)
    done = 0
    for level in range(levels):
        reach = 1 << level
        if level == 0:
            done = (powers - 1) // 2
            lax.fori_loop(0, done, square, 0)

        @pl.when(me < reach)
        def _(level=level):
            current[level + 1] = current[level]

        for part, (start, size) in enumerate(spans):

            @pl.when(me >= reach)
            def _(level=level, part=part, start=start, size=size):
                matrix_copy(level, part).wait_recv()
                joined = dot3(
                    arrived[level, start : start + size, :],
                    split_rhs(current[level, 0:width, :]),
                )
                if part < PIECES - 1:
                    current[level + 1, start : start + size, :] = joined
                else:
                    current[level + 1, start:width, :] = joined[0:piece]
                    current[level + 1, width:, :] = joined[piece:] + current[level, width:, :]

            if level + 1 < levels:
                send_part(level + 1, part)

    chain_copy = pltpu.make_async_remote_copy(
        src_ref=xend, dst_ref=chain, send_sem=chain_send, recv_sem=chain_recv,
        device_id={"tm": lax.rem(me + window, count)}, device_id_type=pl.DeviceIdType.MESH,
    )
    shift_copy = pltpu.make_async_remote_copy(
        src_ref=xend, dst_ref=xin, send_sem=shift_send, recv_sem=shift_recv,
        device_id={"tm": lax.rem(me + 1, count)}, device_id_type=pl.DeviceIdType.MESH,
    )

    def pass_on():
        @pl.when(me + window < count)
        def _():
            chain_copy.start()

        @pl.when(me + 1 < count)
        def _():
            shift_copy.start()

    @pl.when(me < window)
    def _():
        xend[...] = current[levels, width : width + 1, :]
        pass_on()

    def keep(index, carry):
        gsplit[index] = split_rhs(gpow[index])
        return carry

    lax.fori_loop(done, powers - 1, square, 0)
    lax.fori_loop(0, powers, keep, 0)

    @pl.when(me >= window)
    def _():
        chain_copy.wait_recv()
        xend[...] = (
            matvec(chain[...], current[levels, 0:width, :])
            + current[levels, width : width + 1, :]
        )
        pass_on()

    for level in range(levels):
        for part in range(PIECES):

            @pl.when(me + (1 << level) < count)
            def _(level=level, part=part):
                matrix_copy(level, part).wait_send()

    @pl.when(me + window < count)
    def _():
        chain_copy.wait_send()

    @pl.when(me >= 1)
    def _():
        shift_copy.wait_recv()

    @pl.when(me + 1 < count)
    def _():
        shift_copy.wait_send()

    uvec[0] = xin[...] * damp[0:1]
    for level in range(depth - 1, -1, -1):
        size = 1 << level
        offset = 2 * steps - (2 * steps >> level)

        def descend(index, carry, size=size, offset=offset):
            enter = uvec[2 * size * index]
            left = offset + 2 * index
            uvec[2 * size * index + size] = (
                matvec(enter, node[left, 0:width, :]) + node[left, width : width + 1, :]
            )
            return carry

        trips = steps // (2 * size)
        lax.fori_loop(0, trips, descend, 0, unroll=min(4, trips))

    before = jnp.concatenate([uvec[step] for step in range(steps)], axis=0)
    predicted = exact(before, tt[...]) + first_row * prior
    innovation = y_ref[...] - exact(predicted, ht)
    filtered = predicted + exact(weights * innovation, h)
    f_ref[...] = filtered

    last_row = jnp.where(row_ids == steps - 1, 1.0, 0.0).astype(F32) * is_final
    base = filtered - (1.0 - last_row) * exact(exact(filtered, tt[...]), gpow[0])
    for level in range(depth):
        distance = 1 << level
        later = jnp.concatenate(
            [base[distance:], jnp.zeros((distance, width), F32)], axis=0
        )
        base = base + dot3(later, gsplit[level])
    obuf[...] = base[0:1]
    copies = []
    for rank in range(count - 1):
        copy = pltpu.make_async_remote_copy(
            src_ref=obuf, dst_ref=gath.at[rank], send_sem=o_send.at[rank],
            recv_sem=o_recv.at[rank],
            device_id={"tm": lax.rem(me + 2 * count - 1 - rank, count)},
            device_id_type=pl.DeviceIdType.MESH,
        )
        copies.append(copy)

        @pl.when(me > rank)
        def _(copy=copy):
            copy.start()

    for rank, copy in enumerate(copies):

        @pl.when(me + rank + 1 < count)
        def _(copy=copy):
            copy.wait_recv()

    gathered = jnp.concatenate([gath[rank] for rank in range(gath.shape[0])], axis=0)
    for level in range(span_bits - 1, -1, -1):
        half = 1 << level
        gathered = gathered[0:half] + dot3(gathered[half:], gsplit[depth + level])
    lifted = dot3(gathered, gsplit[0])
    for level in range(depth):
        lifted = jnp.concatenate([dot3(lifted, gsplit[level]), lifted], axis=0)
    s_ref[...] = base + lifted

    for rank, copy in enumerate(copies):

        @pl.when(me > rank)
        def _(copy=copy):
            copy.wait_send()


def per_device(
    observations, obs_weights, damping, transition, obs_matrix, smoother_gain, prior_mean
):
    count = lax.axis_size("tm")
    steps, width = damping.shape
    obs = observations.shape[1]
    span_bits = (count - 1).bit_length()
    levels = min(3, span_bits)
    powers = steps.bit_length() - 1 + span_bits
    vmem = pl.BlockSpec(memory_space=pltpu.VMEM)
    out = jax.ShapeDtypeStruct((steps, width), F32)
    dma = pltpu.SemaphoreType.DMA
    return pl.pallas_call(
        functools.partial(kernel, count),
        out_shape=(out, out),
        in_specs=[vmem] * 7,
        out_specs=(vmem, vmem),
        scratch_shapes=[
            pltpu.VMEM((2 * steps - 1, width + PAD, width), F32),
            pltpu.VMEM((levels + 1, width + PAD, width), F32),
            pltpu.VMEM((levels, width + PAD, width), F32),
            pltpu.VMEM((powers, width, width), F32),
            pltpu.VMEM((powers, 3 * width, width), BF16),
            pltpu.VMEM((width, width), F32),
            pltpu.VMEM((width, obs), F32),
            pltpu.VMEM((3 * obs, width), BF16),
            pltpu.VMEM((steps, width), F32),
            pltpu.VMEM((steps, width), F32),
            pltpu.VMEM((steps, 1, width), F32),
            pltpu.VMEM((1, width), F32),
            pltpu.VMEM((1, width), F32),
            pltpu.VMEM((1, width), F32),
            pltpu.VMEM((1, width), F32),
            pltpu.VMEM((1 << span_bits, 1, width), F32),
            dma((levels, PIECES)), dma((levels, PIECES)),
            dma, dma, dma, dma,
            dma((count - 1,)), dma((count - 1,)),
        ],
        compiler_params=pltpu.CompilerParams(
            collective_id=0, has_side_effects=True, vmem_limit_bytes=56 * 1024 * 1024
        ),
    )(
        observations, obs_weights, damping, transition, obs_matrix, smoother_gain,
        prior_mean[None, :],
    )


def solution(mesh):
    return jax.shard_map(
        per_device,
        mesh=mesh,
        in_specs=(P("tm", None), P("tm", None), P("tm", None), P(), P(), P(), P()),
        out_specs=(P("tm", None), P("tm", None)),
        check_vma=False,
    )
```
